32 devices in a mesh: parts: 2 (over y), clus: 16 (over z, x, core).
Axes of the slice: x: 2, y: 2, z: 4, core: 2. Of those that a mesh axis runs over, the one named last changes fastest.
Arguments:
- density: float32 [32, 512, 1024], P(('parts', 'clus')), parts along dimension 0, may hold values from -6 to 6
- positions: float32 [32, 3, 512], P(('parts', 'clus')), parts along dimension 0, may hold values from -0.36 to 1.36
- area: float32 [32, 512], P(('parts', 'clus')), parts along dimension 0, may hold values from 0.01 to 0.04
- incident: float32 [32, 512, 512], P(('parts', 'clus')), parts along dimension 0, may hold values from -6 to 6
- pair_list: int32 [64], P(('parts', 'clus')), parts along dimension 0, may hold values from 0 to 15, as said below
- pair_count: int32 [32], P(('parts', 'clus')), parts along dimension 0, may hold values from 1 to 2, as said below
Outputs:
- residual: float32 [32, 512, 512], P(('parts', 'clus')), parts along dimension 0
The draws below stay inside these ranges and needn't reach their ends.
There are 2 independent parts, one for each index of `parts`. The reference program is written for one: setup_inputs(seed, part) draws one part's arguments, and reference() takes and returns one part's arrays. A program takes and returns all parts, laid end to end along the dimension named above; each array names one. Nothing has to cross between parts.
Inputs may be any that keep to these rules, and one draw needn't show every extreme that they name: `pair_list`: cluster k lies on device k of clus. Slots 2 q to 2 q + 1 belong to cluster q and name the clusters (q + d) mod 16 for distinct d in 1 .. 3; slots past pair_count[q] are ignored. `pair_count`: some cluster has exactly 2 live pairs.
All inputs are finite; a program needn't handle non-finite values.
Results may differ from the reference program's by a relative error of at most 0.0003.
Values sent between devices are 32-bit elements; how exact they have to be, the bound alone decides.
No kernel may reach another device: no remote copies, remote signals or barrier semaphores. Data moves between devices by JAX's collectives and lax.ppermute only.
A program may use at most 128 MiB of HBM per device.

```python
import math
import jax
import jax.numpy as jnp
from jax import lax

NODES = 16
COLS = 32
CL = 512
REACH = 3
MAXP = 2
CLUSTERS = 16
PAIRS = 32


def draw_positions(key, part):
    center_key, spread_key = jax.random.split(jax.random.fold_in(key, 11))
    extent = jnp.array([1.0, 1.0, 0.25], dtype=jnp.float32)
    center = jax.random.uniform(center_key, (CLUSTERS, 3, 1), dtype=jnp.float32) * extent[None, :, None]
    spread = 0.12 * jax.random.truncated_normal(spread_key, -3.0, 3.0, (CLUSTERS, 3, CL), dtype=jnp.float32)
    return (center + spread).astype(jnp.float32)


def draw_pair_list(key, part):
    owner_keys = jax.random.split(jax.random.fold_in(key, 23), CLUSTERS)
    steps_ahead = jax.vmap(lambda single: jax.random.permutation(single, REACH))(owner_keys)[:, :MAXP] + 1
    owners = jnp.arange(CLUSTERS, dtype=jnp.int32)[:, None]
    return ((owners + steps_ahead) % CLUSTERS).reshape(PAIRS).astype(jnp.int32)


def draw_pair_count(key, part):
    pick_key, peak_key = jax.random.split(jax.random.fold_in(key, 37))
    extra = (jax.random.randint(pick_key, (CLUSTERS,), 0, 4) == 0).astype(jnp.int32)
    counts = 1 + extra * (MAXP - 1)
    peak_device = jax.random.randint(peak_key, (), 0, CLUSTERS)
    return jnp.where(jnp.arange(CLUSTERS) == peak_device, MAXP, counts).astype(jnp.int32)


def block_scale(rng, shape, shards, low, largest):
    loudness = 1.0
    for axis_at, shards_of in shards:
        draws = jax.random.uniform(jax.random.fold_in(jax.random.fold_in(rng, 6), axis_at), (shards_of,), jnp.float32, low / len(shards), largest / len(shards))
        loudness = loudness * jnp.repeat(jnp.exp(draws), shape[axis_at] // shards_of).reshape((-1,) + (1,) * (len(shape) - 1 - axis_at))
    return loudness


def bell_draw(own_key, shape, scale, reach, cuts=(), kind=jnp.bfloat16):
    factor_of = block_scale(own_key, shape, cuts, -0.22, 0.18) if cuts else 1.0
    drawn = jax.random.normal(own_key, shape, jnp.float32) * scale * factor_of
    return jnp.minimum(jnp.maximum(drawn, -reach), reach).astype(kind)


def setup_inputs(seed: int = 0, part: int = 0) -> dict:
    streams_of = jax.random.split(jax.random.key(seed), 7)
    part_splits = jax.random.split(jax.random.fold_in(streams_of[6], part), 7)
    return {
        "density": bell_draw(part_splits[0], (CLUSTERS, CL, NODES * 2 * COLS), 1.0, 6.0, ((0, 16),), jnp.float32),
        "positions": draw_positions(jax.random.fold_in(jax.random.fold_in(streams_of[6], part), 71), part),
        "area": jnp.clip(jnp.exp(math.log(0.04) - 1.3862944 * jax.random.uniform(part_splits[2], (CLUSTERS, CL), jnp.float32) ** block_scale(part_splits[2], (CLUSTERS, CL), ((0, 16),), -0.2, 0.2)), 0.01, 0.04),
        "incident": bell_draw(part_splits[3], (CLUSTERS, CL, NODES * COLS), 1.0, 6.0, ((0, 16),), jnp.float32),
        "pair_list": draw_pair_list(jax.random.fold_in(jax.random.fold_in(streams_of[6], part), 71), part),
        "pair_count": draw_pair_count(jax.random.fold_in(jax.random.fold_in(streams_of[6], part), 71), part),
    }


contour_radius = 0.95
smooth_square = 0.01

def laplace_nodes(node_count):
    angles = 2.0 * math.pi * jnp.arange(node_count, dtype=jnp.float32) / node_count
    real_part = 1.0 - contour_radius * jnp.cos(angles)
    imag_part = contour_radius * jnp.sin(angles)
    node_real = real_part + 0.5 * (real_part * real_part - imag_part * imag_part)
    node_imag = imag_part + real_part * imag_part
    return (node_real, node_imag)

def kernel_block(target_place, source_place, node_real, node_imag):
    offset = target_place[:, :, None] - source_place[:, None, :]
    distance = jnp.sqrt(lax.optimization_barrier(jnp.sum(offset * offset, axis=0)) + smooth_square)
    decays = jnp.exp(-node_real[:, None, None] * distance[None]) / distance[None]
    phases = node_imag[:, None, None] * distance[None]
    return (decays * jnp.cos(phases), -decays * jnp.sin(phases))

def apply_block(kernel_real, kernel_imag, source, form):
    panels = source.shape[0]
    node_count = kernel_real.shape[0]
    stacked = source.reshape(panels, node_count, -1)
    half_width = stacked.shape[2] // 2
    real_term = jnp.einsum(form, kernel_real, stacked, precision=lax.Precision.HIGHEST)
    imag_term = jnp.einsum(form, kernel_imag, stacked, precision=lax.Precision.HIGHEST)
    out_real = real_term[..., :half_width] - imag_term[..., half_width:]
    out_imag = real_term[..., half_width:] + imag_term[..., :half_width]
    return jnp.concatenate([out_real, out_imag], axis=2).reshape(panels, -1)

def time_table(node_count, columns):
    row_ids = jnp.arange(node_count * 2 * columns, dtype=jnp.int32)
    col_ids = jnp.arange(node_count * columns, dtype=jnp.int32)
    node_of = row_ids // (2 * columns)
    part_of = row_ids // columns % 2
    column_of = row_ids % columns
    step_of = col_ids // columns
    target_col = col_ids % columns
    product = node_of[:, None] * step_of[None, :] % node_count
    angles = 2.0 * math.pi * product.astype(jnp.float32) / node_count
    waves = jnp.where(part_of[:, None] == 0, jnp.cos(angles), jnp.sin(angles))
    step_scale = jnp.exp(-step_of.astype(jnp.float32) * math.log(contour_radius)) / node_count
    same_column = (column_of[:, None] == target_col[None, :]).astype(jnp.float32)
    return waves * step_scale[None, :] * same_column

def to_time(near_field, time_matrix):
    flattened = near_field.reshape(-1, time_matrix.shape[0])
    result = jnp.dot(flattened, time_matrix, precision=lax.Precision.HIGHEST, preferred_element_type=jnp.float32)
    return result.reshape(near_field.shape[0], near_field.shape[1], -1)

def reference(density, positions, area, incident, pair_list, pair_count):
    node_real, node_imag = laplace_nodes(NODES)
    weighted = density * area[:, :, None]

    def self_term(operands):
        own_place, source = operands
        kernel_real, kernel_imag = kernel_block(own_place, own_place, node_real, node_imag)
        return apply_block(kernel_real, kernel_imag, source, 'lij,jlk->ilk')
    near_field = lax.map(self_term, (positions, weighted))
    slot_ids = jnp.arange(PAIRS, dtype=jnp.int32)
    owners = (slot_ids // MAXP).astype(jnp.int32)
    live = slot_ids % MAXP < pair_count[owners]

    def with_pair(near_field, target, source):
        kernel_real, kernel_imag = kernel_block(positions[target], positions[source], node_real, node_imag)
        forward = apply_block(kernel_real, kernel_imag, weighted[source], 'lij,jlk->ilk')
        backward = apply_block(kernel_real, kernel_imag, weighted[target], 'lij,ilk->jlk')
        near_field = near_field.at[target].add(forward)
        return near_field.at[source].add(backward)

    def add_pair(near_field, operands):
        target, source, live_flag = operands
        near_field = lax.cond(live_flag, lambda held: with_pair(held, target, source), lambda held: held, near_field)
        return (near_field, target)
    near_field, unused = lax.scan(add_pair, near_field, (owners, pair_list, live))
    time_matrix = time_table(NODES, COLS)
    return incident - to_time(near_field, time_matrix)
```

```python
import math

import jax
import jax.numpy as jnp
import numpy as np
from jax import lax
from jax.experimental import pallas as pl
from jax.experimental.pallas import tpu as pltpu
from jax.sharding import PartitionSpec as P

COLS = 32
RADIUS = 0.95
SMOOTH = 0.01
TERMS = 23
SPAN = 4 * COLS
TILE_I = 256
TILE_J = 128
FLAG_ROW = 3
META = 8
F32 = jnp.float32
BF16 = jnp.bfloat16
VMEM_LIMIT = 60 * 1024 * 1024


def residue_map():
    eye = np.eye(16)
    plus, minus = eye[:8] + eye[8:], eye[:8] - eye[8:]
    rows = [plus[m] + plus[m + 4] for m in range(4)]
    rows += [plus[m] - plus[m + 4] for m in range(4)]
    w = np.exp(0.25j * np.pi)
    e = minus[:4] + 1j * minus[4:]
    for sign in (1.0, -1.0):
        pair = [e[m] + sign * w * e[m + 2] for m in range(2)]
        rows += [pair[0].real, pair[1].real, pair[0].imag, pair[1].imag]
    return np.stack(rows)


def fold_table():
    steps = np.arange(16)
    angles = 2.0 * np.pi * (np.outer(steps, steps) % 16) / 16
    fold = np.stack([np.cos(angles), -np.sin(angles)], axis=2).reshape(16, 32) / 16
    table = np.kron(residue_map() @ fold, np.eye(COLS)).astype(np.float32)
    high = table.astype(jnp.bfloat16)
    low = (table - high.astype(np.float32)).astype(jnp.bfloat16)
    return high, low


def scales():
    inv = [1.0] * (TERMS + 1)
    for n in range(3, TERMS):
        inv[n + 1] = inv[n] * 2.0 * RADIUS / (n + 1)
    return inv


def split(value):
    high = value.astype(BF16)
    return high, (value - high.astype(F32)).astype(BF16)


def dot_nt(left, right):
    return lax.dot_general(left, right, (((1,), (1,)), ((), ())), preferred_element_type=F32)


def live_ahead(listed, count, delta):
    devices = lax.axis_size("clus")
    wanted = lax.rem(lax.axis_index("clus") + delta + devices, devices)
    first = (listed[0] == wanted) & (count[0] > 0)
    second = (listed[1] == wanted) & (count[0] > 1)
    return first | second


def fold_kernel(density, area, place, listed, count, high, low, out, own):
    part_high, part_low = split(density[0])
    folded = dot_nt(high[...], part_high) + dot_nt(high[...], part_low) + dot_nt(low[...], part_high)
    rows = folded.shape[0]
    out[0:rows, :] = folded * area[...]
    for axis in range(3):
        out[rows + axis : rows + axis + 1, :] = place[axis]
    for ahead in range(1, 4):
        flag = jnp.where(live_ahead(listed, count, ahead), 1.0, 0.0).astype(F32)
        row = rows + FLAG_ROW + ahead - 1
        out[row : row + 1, :] = jnp.full((1, out.shape[1]), flag, F32)
    out[rows + 6 : rows + 8, :] = jnp.zeros((2, out.shape[1]), F32)
    panels = out.shape[1]
    for axis in range(3):
        spread = jnp.broadcast_to(place[axis], (128, panels))
        own[axis] = spread.T


def kernels(targets, sources):
    inv = scales()
    gaps = [a - b for a, b in zip(targets, sources)]
    square = gaps[0] * gaps[0] + gaps[1] * gaps[1] + gaps[2] * gaps[2] + SMOOTH
    inverse = lax.rsqrt(square)
    dist = square * inverse
    t = [jnp.exp(-1.5 * dist) * inverse]
    t.append((2.0 * RADIUS) * dist * t[0])
    for n in range(1, 3):
        t.append(dist * ((2.0 * RADIUS / (n + 1)) * t[n] - (RADIUS * RADIUS / (n + 1)) * t[n - 1]))
    for n in range(3, TERMS):
        factor = RADIUS * inv[n - 1] / (2.0 * inv[n])
        t.append(dist * (t[n] - factor * t[n - 1]))
    plus, minus = [], []
    for m in range(8):
        base = t[m]
        if m + 16 <= TERMS:
            base = base + (inv[m + 16] / inv[m]) * t[m + 16]
        other = (inv[m + 8] / inv[m]) * t[m + 8]
        plus.append(base + other)
        minus.append(base - other)
    first, second = [], []
    for m in range(4):
        other = inv[m + 4] * plus[m + 4]
        first.append(plus[m] + other)
        second.append(plus[m] - other)
    third, fourth = [], []
    half = math.sqrt(0.5)
    for m in range(2):
        a = half * minus[m + 2]
        b = (half * inv[m + 6]) * minus[m + 6]
        imag = inv[m + 4] * minus[m + 4]
        third += [minus[m] + (a - b), imag + (a + b)]
        fourth += [minus[m] - (a - b), imag - (a + b)]
    return first + second + third + fourth


def prepare(slot, payload, lhs, spots):
    panels = payload.shape[1]
    half = math.sqrt(0.5)
    rows = 16 * COLS
    for j in range(panels // TILE_J):
        at = slice(j * TILE_J, (j + 1) * TILE_J)
        spots[slot, j] = payload[rows : rows + META, at]

        def block(index):
            return payload[index * COLS : (index + 1) * COLS, at]

        def put(group, kernel, position, pieces):
            lanes = slice(kernel * TILE_J, (kernel + 1) * TILE_J)
            top = position * COLS
            lhs[slot, group, j, top : top + COLS, lanes] = pieces[0]
            lhs[slot, group, j, SPAN + top : SPAN + top + COLS, lanes] = pieces[1]

        def minus(pieces):
            return (-pieces[0], -pieces[1])

        for group in range(2):
            pieces = [split(block(group * 4 + n)) for n in range(4)]
            flipped = [minus(p) for p in pieces] if group else pieces
            for k in range(4):
                for n in range(4):
                    put(group, k, n, pieces[n - k] if n >= k else flipped[n - k + 4])
        for group in range(2, 4):
            raw = [block(group * 4 + n) for n in range(4)]
            x0r, x1r, x0i, x1i = [split(r) for r in raw]
            sign = half if group == 2 else -half
            wr = split(sign * (raw[1] - raw[3]))
            wi = split(sign * (raw[1] + raw[3]))
            table = (
                (x0r, x1r, x0i, x1i),
                (minus(x0i), minus(x1i), x0r, x1r),
                (wr, x0r, wi, x0i),
                (minus(wi), minus(x0i), wr, x0r),
            )
            for k in range(4):
                for n in range(4):
                    put(group, k, n, table[k][n])


def near_kernel(offsets, has_input, *refs):
    count = len(offsets)
    listed, live_count, own = refs[:3]
    payloads = refs[3 : 3 + count]
    rest = refs[3 + count :]
    turn = 1 - 2 * lax.rem(lax.axis_index("clus"), 2)
    if has_input:
        rest = rest[1:]
    out, acc, lhs, spots, high0, low0, high1, low1 = rest
    acc[:, SPAN : 2 * SPAN, :] = jnp.zeros((4, SPAN, acc.shape[2]), F32)
    acc[:, 0:SPAN, :] = refs[3 + count][...] if has_input else jnp.zeros((4, SPAN, acc.shape[2]), F32)
    high1[...] = jnp.zeros_like(high1)
    low1[...] = jnp.zeros_like(low1)
    rows = 16 * COLS
    total = jnp.int32(0)
    for s in range(count):
        delta = offsets[s][0] + offsets[s][1] * turn
        ahead = live_ahead(listed, live_count, delta)
        row = rows + FLAG_ROW - 1 + jnp.clip(-delta, 1, 3)
        flag = jnp.max(payloads[s][pl.ds(row, 1), :])
        live = (delta == 0) | ((delta > 0) & ahead) | ((delta < 0) & (flag > 0.5))

        @pl.when(live)
        def _():
            prepare(total, payloads[s], lhs, spots)

        total = total + live.astype(jnp.int32)

    def evaluate(slot, j, i, high, low, quarter):
        step = TILE_I // 4
        spot = spots[slot, j]
        sources = [jnp.broadcast_to(spot[a : a + 1, :], (16, TILE_J)) for a in range(3)]
        for r in range(quarter * step, (quarter + 1) * step, 16):
            targets = [own[a, i * TILE_I + r : i * TILE_I + r + 16, :] for a in range(3)]
            for index, value in enumerate(kernels(targets, sources)):
                top, bottom = split(value)
                lanes = slice((index % 4) * TILE_J, (index % 4 + 1) * TILE_J)
                high[index // 4, r : r + 16, lanes] = top
                low[index // 4, r : r + 16, lanes] = bottom

    def apply(slot, j, i, high, low, group):
        left = lhs[slot, group, j]
        at = slice(i * TILE_I, (i + 1) * TILE_I)
        acc[group, :, at] += dot_nt(left, high[group])
        acc[group, 0:SPAN, at] += dot_nt(left[0:SPAN], low[group])

    tiles = own.shape[1] // TILE_J

    def step(index, carry):
        slot, j = index // tiles, index % tiles
        before = jnp.maximum(index - 1, 0)
        slot_before, j_before = before // tiles, before % tiles
        for quarter in range(4):
            evaluate(slot, j, 0, high0, low0, quarter)
            apply(slot_before, j_before, 1, high1, low1, quarter)
        for quarter in range(4):
            evaluate(slot, j, 1, high1, low1, quarter)
            apply(slot, j, 0, high0, low0, quarter)
        return carry

    lax.fori_loop(0, total * tiles, step, 0)

    @pl.when(total > 0)
    def _():
        for group in range(4):
            apply(total - 1, tiles - 1, 1, high1, low1, group)

    out[...] = acc[:, 0:SPAN, :] + acc[:, SPAN : 2 * SPAN, :]


def near_call(pairs, own, offsets, payloads, acc):
    count = len(payloads)
    panels = own.shape[1]
    tiles = panels // TILE_J
    shape = jax.ShapeDtypeStruct((4, SPAN, panels), F32)
    vmem = pl.BlockSpec(memory_space=pltpu.VMEM)
    smem = pl.BlockSpec(memory_space=pltpu.SMEM)
    arguments = [*pairs, own, *payloads] + ([] if acc is None else [acc])
    return pl.pallas_call(
        lambda *refs: near_kernel(offsets, acc is not None, *refs),
        out_shape=shape,
        in_specs=[smem] * 2 + [vmem] * (len(arguments) - 2),
        out_specs=vmem,
        scratch_shapes=[
            pltpu.VMEM((4, 2 * SPAN, panels), F32),
            pltpu.VMEM((count, 4, tiles, 2 * SPAN, 4 * TILE_J), BF16),
            pltpu.VMEM((count, tiles, META, TILE_J), F32),
        ]
        + [pltpu.VMEM((4, TILE_I, 4 * TILE_J), BF16)] * 4,
        compiler_params=pltpu.CompilerParams(vmem_limit_bytes=VMEM_LIMIT),
        cost_estimate=pl.CostEstimate(
            flops=count * 2 * 32768 * 256 * 256 // 2, bytes_accessed=4 << 20, transcendentals=0
        ),
        name="near",
    )(*arguments)


def final_kernel(acc, incident, out):
    panels = acc.shape[2]
    half = math.sqrt(0.5)
    for lane in range(0, panels, 128):
        at = slice(lane, lane + 128)
        parts = []
        for group in range(4):
            whole = acc[group, :, at]
            parts.append([whole[n * COLS : (n + 1) * COLS] for n in range(4)])
        first, second, third, fourth = parts
        plus = [first[n] + second[n] for n in range(4)] + [first[n] - second[n] for n in range(4)]
        minus = [None] * 8
        for m in range(2):
            sum_r, sum_i = third[m] + fourth[m], third[m + 2] + fourth[m + 2]
            gap_r, gap_i = third[m] - fourth[m], third[m + 2] - fourth[m + 2]
            minus[m], minus[m + 4] = sum_r, sum_i
            minus[m + 2] = half * (gap_r + gap_i)
            minus[m + 6] = half * (gap_i - gap_r)
        steps = [None] * 16
        for m in range(8):
            low = plus[m] + minus[m]
            high = plus[m] - minus[m]
            for n, value in ((-m % 16, low), ((-m - 8) % 16, high)):
                steps[n] = value * (0.25 * RADIUS ** (-n))
        potential = jnp.concatenate(steps, axis=0).T
        out[0, at, :] = incident[0, at, :] - potential


def residual(density, positions, area, incident, pair_list, pair_count):
    devices = lax.axis_size("clus")
    panels = positions.shape[2]
    pairs = (pair_list, pair_count)
    table_high, table_low = fold_table()
    vmem = pl.BlockSpec(memory_space=pltpu.VMEM)
    smem = pl.BlockSpec(memory_space=pltpu.SMEM)
    payload, own = pl.pallas_call(
        fold_kernel,
        out_shape=(
            jax.ShapeDtypeStruct((16 * COLS + META, panels), F32),
            jax.ShapeDtypeStruct((3, panels, 128), F32),
        ),
        in_specs=[vmem, vmem, vmem, smem, smem, vmem, vmem],
        out_specs=(vmem, vmem),
        compiler_params=pltpu.CompilerParams(vmem_limit_bytes=VMEM_LIMIT),
        name="fold",
    )(density, area, positions.transpose(1, 0, 2), *pairs, jnp.asarray(table_high), jnp.asarray(table_low))

    def route(value, move, members=lambda k: True):
        pairs_of = [(k, move(k) % devices) for k in range(devices) if members(k)]
        return lax.ppermute(value, "clus", pairs_of)

    def swap(value):
        return route(value, lambda k: k ^ 1)

    partner = swap(payload)
    ahead = route(payload, lambda k: k - 2)
    far = route(payload, lambda k: k - 3 if k % 2 == 0 else k + 3)
    behind = route(payload, lambda k: k + 2)
    acc = near_call(pairs, own, ((0, 0), (0, 1)), (payload, partner), None)
    ahead_other = swap(ahead)
    acc = near_call(pairs, own, ((2, 0),), (ahead,), acc)
    acc = near_call(pairs, own, ((2, 1), (0, -3)), (ahead_other, far), acc)
    behind_other = swap(behind)
    acc = near_call(pairs, own, ((-2, 0),), (behind,), acc)
    acc = near_call(pairs, own, ((-2, 1),), (behind_other,), acc)
    return pl.pallas_call(
        final_kernel,
        out_shape=jax.ShapeDtypeStruct(incident.shape, F32),
        in_specs=[vmem, vmem],
        out_specs=vmem,
        compiler_params=pltpu.CompilerParams(vmem_limit_bytes=VMEM_LIMIT),
        name="final",
    )(acc, incident)


def solution(mesh):
    spec3 = P(("parts", "clus"), None, None)
    in_specs = (spec3, spec3, P(("parts", "clus"), None), spec3, P(("parts", "clus")), P(("parts", "clus")))
    return jax.shard_map(residual, mesh=mesh, in_specs=in_specs, out_specs=spec3, check_vma=False)
```

```python
import math

import jax
import jax.numpy as jnp
import numpy as np
from jax import lax
from jax.experimental import pallas as pl
from jax.experimental.pallas import tpu as pltpu
from jax.sharding import PartitionSpec as P

COLS = 32
RADIUS = 0.95
SMOOTH = 0.01
TERMS = 23
SPAN = 4 * COLS
TILE_I = 256
TILE_J = 256
LANES = 128
KPART = 4
FLAG_ROW = 3
META = 8
F32 = jnp.float32
BF16 = jnp.bfloat16
VMEM_LIMIT = 60 * 1024 * 1024
NEAR_LIMIT = 67043328


def residue_map():
    eye = np.eye(16)
    plus, minus = eye[:8] + eye[8:], eye[:8] - eye[8:]
    rows = [plus[m] + plus[m + 4] for m in range(4)]
    rows += [plus[m] - plus[m + 4] for m in range(4)]
    w = np.exp(0.25j * np.pi)
    e = minus[:4] + 1j * minus[4:]
    for sign in (1.0, -1.0):
        pair = [e[m] + sign * w * e[m + 2] for m in range(2)]
        rows += [pair[0].real, pair[1].real, pair[0].imag, pair[1].imag]
    return np.stack(rows)


def fold_table():
    steps = np.arange(16)
    angles = 2.0 * np.pi * (np.outer(steps, steps) % 16) / 16
    fold = np.stack([np.cos(angles), -np.sin(angles)], axis=2).reshape(16, 32) / 16
    table = np.kron(residue_map() @ fold, np.eye(COLS)).astype(np.float32)
    high = table.astype(jnp.bfloat16)
    low = (table - high.astype(np.float32)).astype(jnp.bfloat16)
    return high, low


def scales():
    inv = [1.0] * (TERMS + 1)
    for n in range(3, TERMS):
        inv[n + 1] = inv[n] * 2.0 * RADIUS / (n + 1)
    return inv


def split(value):
    high = value.astype(BF16)
    return high, (value - high.astype(F32)).astype(BF16)


def dot_nt(left, right):
    return lax.dot_general(left, right, (((1,), (1,)), ((), ())), preferred_element_type=F32)


def live_ahead(listed, count, delta):
    devices = lax.axis_size("clus")
    wanted = lax.rem(lax.axis_index("clus") + delta + devices, devices)
    first = (listed[0] == wanted) & (count[0] > 0)
    second = (listed[1] == wanted) & (count[0] > 1)
    return first | second


def fold_kernel(density, area, place, listed, count, high, low, out, own):
    part_high, part_low = split(density[0])
    folded = dot_nt(high[...], part_high) + dot_nt(high[...], part_low) + dot_nt(low[...], part_high)
    rows = folded.shape[0]
    out[0:rows, :] = folded * area[...]
    for axis in range(3):
        out[rows + axis : rows + axis + 1, :] = place[axis]
    for ahead in range(1, 4):
        flag = jnp.where(live_ahead(listed, count, ahead), 1.0, 0.0).astype(F32)
        row = rows + FLAG_ROW + ahead - 1
        out[row : row + 1, :] = jnp.full((1, out.shape[1]), flag, F32)
    out[rows + 6 : rows + 8, :] = jnp.zeros((2, out.shape[1]), F32)
    panels = out.shape[1]
    for axis in range(3):
        spread = jnp.broadcast_to(place[axis], (128, panels))
        own[axis] = spread.T


def kernels(targets, sources):
    inv = scales()
    gaps = [a - b for a, b in zip(targets, sources)]
    square = gaps[0] * gaps[0] + gaps[1] * gaps[1] + gaps[2] * gaps[2] + SMOOTH
    inverse = lax.rsqrt(square)
    dist = square * inverse
    t = [jnp.exp(-1.5 * dist) * inverse]
    t.append((2.0 * RADIUS) * dist * t[0])
    for n in range(1, 3):
        t.append(dist * ((2.0 * RADIUS / (n + 1)) * t[n] - (RADIUS * RADIUS / (n + 1)) * t[n - 1]))
    for n in range(3, TERMS):
        factor = RADIUS * inv[n - 1] / (2.0 * inv[n])
        t.append(dist * (t[n] - factor * t[n - 1]))
    plus, minus = [], []
    for m in range(8):
        base = t[m]
        if m + 16 <= TERMS:
            base = base + (inv[m + 16] / inv[m]) * t[m + 16]
        other = (inv[m + 8] / inv[m]) * t[m + 8]
        plus.append(base + other)
        minus.append(base - other)
    first, second = [], []
    for m in range(4):
        other = inv[m + 4] * plus[m + 4]
        first.append(plus[m] + other)
        second.append(plus[m] - other)
    third, fourth = [], []
    half = math.sqrt(0.5)
    for m in range(2):
        a = half * minus[m + 2]
        b = (half * inv[m + 6]) * minus[m + 6]
        imag = inv[m + 4] * minus[m + 4]
        third += [minus[m] + (a - b), imag + (a + b)]
        fourth += [minus[m] - (a - b), imag - (a + b)]
    return first + second + third + fourth


def prepare(slot, payload, lhs, spots):
    panels = payload.shape[1]
    half = math.sqrt(0.5)
    rows = 16 * COLS

    def column(j, carry):
        at = pl.ds(pl.multiple_of(j * LANES, LANES), LANES)
        spots[slot, j] = payload[rows : rows + META, at]

        def block(index, part):
            top = index * COLS + part * 16
            return payload[top : top + 16, at]

        def put(kernel, position, part, pieces):
            top = position * COLS + part * 16
            lhs[slot, kernel, j, top : top + 16, :] = pieces[0]
            lhs[slot, kernel, j, SPAN + top : SPAN + top + 16, :] = pieces[1]

        for group in range(4):
            for part in range(COLS // 16):
                raw = [block(group * 4 + n, part) for n in range(4)]
                if group < 2:
                    pieces = [split(r) for r in raw]
                    flipped = [split(-r) for r in raw] if group else pieces
                    table = [
                        [pieces[n - k] if n >= k else flipped[n - k + 4] for n in range(4)]
                        for k in range(4)
                    ]
                else:
                    sign = half if group == 2 else -half
                    x0r, x1r, x0i, x1i = [split(r) for r in raw]
                    n0i, n1i = split(-raw[2]), split(-raw[3])
                    turned = sign * (raw[1] + raw[3])
                    wr, wi, nwi = split(sign * (raw[1] - raw[3])), split(turned), split(-turned)
                    table = [
                        [x0r, x1r, x0i, x1i],
                        [n0i, n1i, x0r, x1r],
                        [wr, x0r, wi, x0i],
                        [nwi, n0i, wr, x0r],
                    ]
                for k in range(4):
                    for n in range(4):
                        put(group * 4 + k, n, part, table[k][n])
        return carry

    lax.fori_loop(0, panels // LANES, column, 0)


def near_kernel(offsets, has_input, *refs):
    count = len(offsets)
    listed, live_count, own_hbm = refs[:3]
    payload_hbm = refs[3 : 3 + count]
    rest = refs[3 + count :]
    before_hbm = rest[0] if has_input else None
    out_hbm, payloads, own, acc, lhs, spots, high0, low0, high1, low1, sems = rest[-11:]
    turn = 1 - 2 * lax.rem(lax.axis_index("clus"), 2)
    loads = [
        pltpu.make_async_copy(payload_hbm[s], payloads.at[s], sems.at[2 + s]) for s in range(count)
    ]
    for load in loads:
        load.start()
    own_load = pltpu.make_async_copy(own_hbm, own, sems.at[0])
    head = acc.at[:, 0:SPAN, :]
    rows = 16 * COLS
    lives = []
    for s in range(count):
        loads[s].wait()
        delta = offsets[s][0] + offsets[s][1] * turn
        ahead = live_ahead(listed, live_count, delta)
        row = rows + FLAG_ROW - 1 + jnp.clip(-delta, 1, 3)
        flag = jnp.max(payloads[s, pl.ds(row, 1), :])
        live = (delta == 0) | ((delta > 0) & ahead) | ((delta < 0) & (flag > 0.5))
        lives.append(live.astype(jnp.int32))
    total = sum(lives[1:], lives[0])

    @pl.when(total > 0)
    def _():
        near_body(has_input, lives, total, own_load, before_hbm, payloads, own, acc, head, lhs, spots,
                  high0, low0, high1, low1, sems)
        store = pltpu.make_async_copy(head, out_hbm, sems.at[1])
        store.start()
        store.wait()


def near_body(has_input, lives, total, own_load, before_hbm, payloads, own, acc, head, lhs, spots,
              high0, low0, high1, low1, sems):
    own_load.start()
    if has_input:
        before_load = pltpu.make_async_copy(before_hbm, head, sems.at[1])
        before_load.start()
    else:
        head[...] = jnp.zeros(head.shape, F32)
    acc[:, SPAN : 2 * SPAN, :] = jnp.zeros(head.shape, F32)
    high1[...] = jnp.zeros_like(high1)
    low1[...] = jnp.zeros_like(low1)
    slot_of = jnp.int32(0)
    for s, live in enumerate(lives):

        @pl.when(live > 0)
        def _():
            prepare(slot_of, payloads.at[s], lhs, spots)

        slot_of = slot_of + live
    own_load.wait()
    if has_input:
        before_load.wait()
    halves = TILE_J // LANES

    def evaluate(slot, j, i, high, low, quarter):
        steps = KPART
        for r in range(steps):
            row = pl.multiple_of((quarter * steps + r) * 16, 16)
            targets = [own[a, pl.ds(i * TILE_I + row, 16), :] for a in range(3)]
            for h in range(halves):
                spot = spots[slot, j * halves + h]
                sources = [jnp.broadcast_to(spot[a : a + 1, :], (16, LANES)) for a in range(3)]
                values = kernels(targets, sources)
                for index, value in enumerate(values):
                    top, bottom = split(value)
                    high[index, h, pl.ds(row, 16), :] = top
                    low[index, h, pl.ds(row, 16), :] = bottom

    def joined(read):
        return jnp.concatenate([read(k, h) for k in range(KPART) for h in range(halves)], axis=1)

    def apply(slot, j, i, high, low, part):
        first = part * KPART
        group = first // 4
        left = joined(lambda k, h: lhs[slot, first + k, j * halves + h])
        at = slice(i * TILE_I, (i + 1) * TILE_I)
        acc[group, :, at] += dot_nt(left, joined(lambda k, h: high[first + k, h]))
        acc[group, 0:SPAN, at] += dot_nt(left[0:SPAN], joined(lambda k, h: low[first + k, h]))

    tiles = own.shape[1] // TILE_J

    def step(index, carry):
        slot, j = index // tiles, index % tiles
        before = jnp.maximum(index - 1, 0)
        slot_before, j_before = before // tiles, before % tiles

        def first(r, c):
            evaluate(slot, j, 0, high0, low0, r)
            apply(slot_before, j_before, 1, high1, low1, r)
            return c

        def second(r, c):
            evaluate(slot, j, 1, high1, low1, r)
            apply(slot, j, 0, high0, low0, r)
            return c

        lax.fori_loop(0, 16 // KPART, first, 0)
        lax.fori_loop(0, 16 // KPART, second, 0)
        return carry

    lax.fori_loop(0, total * tiles, step, 0)

    def last(part, c):
        apply(total - 1, tiles - 1, 1, high1, low1, part)
        return c

    lax.fori_loop(0, 16 // KPART, last, 0)
    head[...] = acc[:, 0:SPAN, :] + acc[:, SPAN : 2 * SPAN, :]


def near_call(pairs, own, offsets, payloads, acc):
    count = len(payloads)
    panels = own.shape[1]
    tiles = panels // LANES
    shape = jax.ShapeDtypeStruct((4, SPAN, panels), F32)
    anywhere = pl.BlockSpec(memory_space=pl.ANY)
    smem = pl.BlockSpec(memory_space=pltpu.SMEM)
    arguments = [*pairs, own, *payloads] + ([] if acc is None else [acc])
    return pl.pallas_call(
        lambda *refs: near_kernel(offsets, acc is not None, *refs),
        out_shape=shape,
        in_specs=[smem] * 2 + [anywhere] * (len(arguments) - 2),
        out_specs=anywhere,
        input_output_aliases={} if acc is None else {len(arguments) - 1: 0},
        scratch_shapes=[
            pltpu.VMEM((count,) + payloads[0].shape, F32),
            pltpu.VMEM(own.shape, F32),
            pltpu.VMEM((4, 2 * SPAN, panels), F32),
            pltpu.VMEM((count, 16, tiles, 2 * SPAN, LANES), BF16),
            pltpu.VMEM((count, tiles, META, LANES), F32),
        ]
        + [pltpu.VMEM((16, TILE_J // LANES, TILE_I, LANES), BF16)] * 4
        + [pltpu.SemaphoreType.DMA((2 + count,))],
        compiler_params=pltpu.CompilerParams(vmem_limit_bytes=NEAR_LIMIT),
        cost_estimate=pl.CostEstimate(
            flops=count * 2 * 32768 * 256 * 256, bytes_accessed=4 << 20, transcendentals=0
        ),
        name="near",
    )(*arguments)


def final_kernel(acc, incident, out):
    panels = acc.shape[2]
    half = math.sqrt(0.5)
    for lane in range(0, panels, 128):
        at = slice(lane, lane + 128)
        parts = []
        for group in range(4):
            whole = acc[group, :, at]
            parts.append([whole[n * COLS : (n + 1) * COLS] for n in range(4)])
        first, second, third, fourth = parts
        plus = [first[n] + second[n] for n in range(4)] + [first[n] - second[n] for n in range(4)]
        minus = [None] * 8
        for m in range(2):
            sum_r, sum_i = third[m] + fourth[m], third[m + 2] + fourth[m + 2]
            gap_r, gap_i = third[m] - fourth[m], third[m + 2] - fourth[m + 2]
            minus[m], minus[m + 4] = sum_r, sum_i
            minus[m + 2] = half * (gap_r + gap_i)
            minus[m + 6] = half * (gap_i - gap_r)
        steps = [None] * 16
        for m in range(8):
            low = plus[m] + minus[m]
            high = plus[m] - minus[m]
            for n, value in ((-m % 16, low), ((-m - 8) % 16, high)):
                steps[n] = value * (0.25 * RADIUS ** (-n))
        potential = jnp.concatenate(steps, axis=0).T
        out[0, at, :] = incident[0, at, :] - potential


def residual(density, positions, area, incident, pair_list, pair_count):
    devices = lax.axis_size("clus")
    panels = positions.shape[2]
    pairs = (pair_list, pair_count)
    table_high, table_low = fold_table()
    vmem = pl.BlockSpec(memory_space=pltpu.VMEM)
    smem = pl.BlockSpec(memory_space=pltpu.SMEM)
    payload, own = pl.pallas_call(
        fold_kernel,
        out_shape=(
            jax.ShapeDtypeStruct((16 * COLS + META, panels), F32),
            jax.ShapeDtypeStruct((3, panels, 128), F32),
        ),
        in_specs=[vmem, vmem, vmem, smem, smem, vmem, vmem],
        out_specs=(vmem, vmem),
        compiler_params=pltpu.CompilerParams(vmem_limit_bytes=VMEM_LIMIT),
        name="fold",
    )(density, area, positions.transpose(1, 0, 2), *pairs, jnp.asarray(table_high), jnp.asarray(table_low))

    def route(value, move, members=lambda k: True):
        pairs_of = [(k, move(k) % devices) for k in range(devices) if members(k)]
        return lax.ppermute(value, "clus", pairs_of)

    def swap(value):
        return route(value, lambda k: k ^ 1)

    partner = swap(payload)
    ahead = route(payload, lambda k: k - 2)
    far = route(payload, lambda k: k - 3 if k % 2 == 0 else k + 3)
    behind = route(payload, lambda k: k + 2)
    acc = near_call(pairs, own, ((0, 0), (0, 1)), (payload, partner), None)
    ahead_other = swap(ahead)
    acc = near_call(pairs, own, ((2, 0), (2, 1)), (ahead, ahead_other), acc)
    behind_other = swap(behind)
    acc = near_call(pairs, own, ((-2, 0), (-2, 1), (0, -3)), (behind, behind_other, far), acc)
    return pl.pallas_call(
        final_kernel,
        out_shape=jax.ShapeDtypeStruct(incident.shape, F32),
        in_specs=[vmem, vmem],
        out_specs=vmem,
        compiler_params=pltpu.CompilerParams(vmem_limit_bytes=VMEM_LIMIT),
        name="final",
    )(acc, incident)


def solution(mesh):
    spec3 = P(("parts", "clus"), None, None)
    in_specs = (spec3, spec3, P(("parts", "clus"), None), spec3, P(("parts", "clus")), P(("parts", "clus")))
    return jax.shard_map(residual, mesh=mesh, in_specs=in_specs, out_specs=spec3, check_vma=False)
```

```python
import math

import jax
import jax.numpy as jnp
import numpy as np
from jax import lax
from jax.experimental import pallas as pl
from jax.experimental.pallas import tpu as pltpu
from jax.sharding import PartitionSpec as P

COLS = 32
RADIUS = 0.95
SMOOTH = 0.01
TERMS = 23
SPAN = 4 * COLS
TILE_I = 256
TILE_J = 256
LANES = 128
KPART = 4
FAR = 7
FOLD = 256
FLAG_ROW = 3
META = 8
F32 = jnp.float32
BF16 = jnp.bfloat16
VMEM_LIMIT = 60 * 1024 * 1024
NEAR_LIMIT = 67043328


def residue_map():
    eye = np.eye(16)
    plus, minus = eye[:8] + eye[8:], eye[:8] - eye[8:]
    rows = [plus[m] + plus[m + 4] for m in range(4)]
    rows += [plus[m] - plus[m + 4] for m in range(4)]
    w = np.exp(0.25j * np.pi)
    e = minus[:4] + 1j * minus[4:]
    for sign in (1.0, -1.0):
        pair = [e[m] + sign * w * e[m + 2] for m in range(2)]
        rows += [pair[0].real, pair[1].real, pair[0].imag, pair[1].imag]
    return np.stack(rows)


def fold_table():
    steps = np.arange(16)
    angles = 2.0 * np.pi * (np.outer(steps, steps) % 16) / 16
    fold = np.stack([np.cos(angles), -np.sin(angles)], axis=2).reshape(16, 32) / 16
    return residue_map() @ fold


def nodes_of(group):
    offset = (0, 2, 1, 3)[group]
    table = np.abs(fold_table()[group * 4 : group * 4 + 4]).reshape(4, 16, 2).max(axis=(0, 2))
    nodes = [l for l in range(16) if table[l] > 1e-9]
    assert len(nodes) == 4 and offset in nodes
    return nodes


def scales():
    inv = [1.0] * (TERMS + 1)
    for n in range(3, TERMS):
        inv[n + 1] = inv[n] * 2.0 * RADIUS / (n + 1)
    return inv


def split(value):
    high = value.astype(BF16)
    return high, (value - high.astype(F32)).astype(BF16)


def dot_nt(left, right):
    return lax.dot_general(left, right, (((1,), (1,)), ((), ())), preferred_element_type=F32)


def live_ahead(listed, count, delta):
    devices = lax.axis_size("clus")
    wanted = lax.rem(lax.axis_index("clus") + delta + devices, devices)
    first = (listed[0] == wanted) & (count[0] > 0)
    second = (listed[1] == wanted) & (count[0] > 1)
    return first | second


def fold_kernel(density, area, place, listed, count, out, turned):
    turned[...] = density[0].T
    table = fold_table()
    for group in range(4):
        nodes = nodes_of(group)
        for n in range(4):
            index = group * 4 + n
            total = None
            for entry in [2 * l + part for l in nodes for part in range(2)]:
                term = float(table[index, entry]) * turned[entry * COLS : (entry + 1) * COLS, :]
                total = term if total is None else total + term
            out[index * COLS : (index + 1) * COLS, :] = total * area[...]
    rows = 16 * COLS
    width = out.shape[1]
    for axis in range(3):
        out[rows + axis : rows + axis + 1, :] = place[axis]
    for ahead in range(1, 4):
        flag = jnp.where(live_ahead(listed, count, ahead), 1.0, 0.0).astype(F32)
        row = rows + FLAG_ROW + ahead - 1
        out[row : row + 1, :] = jnp.full((1, width), flag, F32)
    out[rows + 6 : rows + 8, :] = jnp.zeros((2, width), F32)


def kernels(targets, sources):
    inv = scales()
    gaps = [a - b for a, b in zip(targets, sources)]
    square = gaps[0] * gaps[0] + gaps[1] * gaps[1] + gaps[2] * gaps[2] + SMOOTH
    inverse = lax.rsqrt(square)
    dist = square * inverse
    t = [jnp.exp(-1.5 * dist) * inverse]
    t.append((2.0 * RADIUS) * dist * t[0])
    for n in range(1, 3):
        t.append(dist * ((2.0 * RADIUS / (n + 1)) * t[n] - (RADIUS * RADIUS / (n + 1)) * t[n - 1]))
    for n in range(3, TERMS):
        factor = RADIUS * inv[n - 1] / (2.0 * inv[n])
        t.append(dist * (t[n] - factor * t[n - 1]))
    plus, minus = [], []
    for m in range(8):
        base = t[m]
        if m + 16 <= TERMS:
            base = base + (inv[m + 16] / inv[m]) * t[m + 16]
        other = (inv[m + 8] / inv[m]) * t[m + 8]
        plus.append(base + other)
        minus.append(base - other)
    first, second = [], []
    for m in range(4):
        other = inv[m + 4] * plus[m + 4]
        first.append(plus[m] + other)
        second.append(plus[m] - other)
    third, fourth = [], []
    half = math.sqrt(0.5)
    for m in range(2):
        a = half * minus[m + 2]
        b = (half * inv[m + 6]) * minus[m + 6]
        imag = inv[m + 4] * minus[m + 4]
        third += [minus[m] + (a - b), imag + (a + b)]
        fourth += [minus[m] - (a - b), imag - (a + b)]
    return first + second + third + fourth


def prepare(slot, payload, lhs, spots):
    panels = payload.shape[1]
    half = math.sqrt(0.5)
    rows = 16 * COLS

    def column(j, carry):
        at = pl.ds(pl.multiple_of(j * LANES, LANES), LANES)
        spots[slot, j] = payload[rows : rows + META, at]

        def block(index, part):
            top = index * COLS + part * 16
            return payload[top : top + 16, at]

        def put(kernel, position, part, pieces):
            top = position * COLS + part * 16
            lhs[slot, kernel, j, top : top + 16, :] = pieces[0]
            lhs[slot, kernel, j, SPAN + top : SPAN + top + 16, :] = pieces[1]

        for group in range(4):
            for part in range(COLS // 16):
                raw = [block(group * 4 + n, part) for n in range(4)]
                if group < 2:
                    pieces = [split(r) for r in raw]
                    flipped = [split(-r) for r in raw] if group else pieces
                    table = [
                        [pieces[n - k] if n >= k else flipped[n - k + 4] for n in range(4)]
                        for k in range(4)
                    ]
                else:
                    sign = half if group == 2 else -half
                    x0r, x1r, x0i, x1i = [split(r) for r in raw]
                    n0i, n1i = split(-raw[2]), split(-raw[3])
                    turned = sign * (raw[1] + raw[3])
                    wr, wi, nwi = split(sign * (raw[1] - raw[3])), split(turned), split(-turned)
                    table = [
                        [x0r, x1r, x0i, x1i],
                        [n0i, n1i, x0r, x1r],
                        [wr, x0r, wi, x0i],
                        [nwi, n0i, wr, x0r],
                    ]
                for k in range(4):
                    for n in range(4):
                        put(group * 4 + k, n, part, table[k][n])
        return carry

    lax.fori_loop(0, panels // LANES, column, 0)


def near_kernel(sources, has_input, last, *refs):
    count = len(sources)
    regions = 3 if last else 2
    metas_hbm = refs[0:2]
    payload_hbm = refs[2 : 2 + count]
    rest = refs[2 + count :]
    before_hbm = rest[0] if has_input else None
    outs = rest[1:] if has_input else rest
    payloads, metas, own, acc, lhs, spots, high0, low0, high1, low1, items, sems = outs[-12:]
    outs = outs[:-12]
    core = lax.rem(lax.axis_index("clus"), 2)
    rows = 16 * COLS
    head = acc.at[:, 0:SPAN, 0 : 2 * TILE_I]
    loads = [
        pltpu.make_async_copy(payload_hbm[s], payloads.at[s], sems.at[4 + s]) for s in range(count)
    ]
    info = [
        pltpu.make_async_copy(
            metas_hbm[m].at[pl.ds(rows, META), :], metas.at[core if m == 0 else 1 - core], sems.at[2 + m]
        )
        for m in range(2)
    ]
    for load in info + loads:
        load.start()
    for load in info + loads:
        load.wait()

    def flag(meta, distance):
        row = FLAG_ROW - 1 + jnp.clip(distance, 1, 3)
        return (jnp.max(meta(row)) > 0.5) & (distance >= 1) & (distance <= 3)

    total = jnp.int32(0)
    used = []
    for s, (base, slope) in enumerate(sources):
        lives = []
        for t in range(2):
            delta = base + slope * core - t
            ahead = flag(lambda row: metas[t, pl.ds(row, 1), :], delta)
            behind = flag(lambda row: payloads[s, pl.ds(rows + row, 1), :], -delta)
            lives.append((delta == 0) | ahead | behind)
        used.append(lives[0] | lives[1])
        if slope == FAR:
            lives.append(used[-1])
        for region, live in enumerate(lives):

            @pl.when(live)
            def _():
                items[0, total] = s
                items[1, total] = region

            total = total + live.astype(jnp.int32)

    def body():
        if has_input:
            before_load = pltpu.make_async_copy(before_hbm, head, sems.at[0])
            before_load.start()
        else:
            head[...] = jnp.zeros(head.shape, F32)
        if last:
            acc[:, 0:SPAN, 2 * TILE_I :] = jnp.zeros((4, SPAN, TILE_I), F32)
        acc[:, SPAN : 2 * SPAN, :] = jnp.zeros((4, SPAN, regions * TILE_I), F32)
        high1[...] = jnp.zeros_like(high1)
        low1[...] = jnp.zeros_like(low1)
        for region in range(regions):
            cluster = core if region == 2 else region
            side = 1 - core if region == 2 else core
            at = pl.ds(pl.multiple_of(side * TILE_I, TILE_I), TILE_I)
            for axis in range(3):
                line = metas[cluster, axis : axis + 1, at]
                own[axis, region * TILE_I : (region + 1) * TILE_I, :] = jnp.broadcast_to(line, (LANES, TILE_I)).T
        for s in range(count):

            @pl.when(used[s])
            def _():
                prepare(s, payloads.at[s], lhs, spots)

        if has_input:
            before_load.wait()
        near_body(total, own, acc, lhs, spots, high0, low0, high1, low1, items)
        acc[:, 0:SPAN, :] = acc[:, 0:SPAN, :] + acc[:, SPAN : 2 * SPAN, :]

    if last:
        body()

        def region_of(index):
            return acc.at[:, 0:SPAN, pl.ds(pl.multiple_of(index * TILE_I, TILE_I), TILE_I)]

        keep, send = outs
        stores = [
            pltpu.make_async_copy(region_of(core), keep.at[:, :, 0:TILE_I], sems.at[0]),
            pltpu.make_async_copy(region_of(2), keep.at[:, :, TILE_I : 2 * TILE_I], sems.at[1]),
            pltpu.make_async_copy(region_of(1 - core), send, sems.at[2]),
        ]
        for store in stores:
            store.start()
        for store in stores:
            store.wait()
    else:

        @pl.when(total > 0)
        def _():
            body()
            store = pltpu.make_async_copy(head, outs[0], sems.at[1])
            store.start()
            store.wait()


def near_body(total, own, acc, lhs, spots, high0, low0, high1, low1, items):
    halves = TILE_J // LANES

    def evaluate(slot, j, region, high, low, quarter):
        for r in range(KPART):
            row = pl.multiple_of((quarter * KPART + r) * 16, 16)
            at = pl.multiple_of(region * TILE_I + row, 16)
            targets = [own[a, pl.ds(at, 16), :] for a in range(3)]
            for h in range(halves):
                spot = spots[slot, j * halves + h]
                sources = [jnp.broadcast_to(spot[a : a + 1, :], (16, LANES)) for a in range(3)]
                for index, value in enumerate(kernels(targets, sources)):
                    top, bottom = split(value)
                    high[index, h, pl.ds(row, 16), :] = top
                    low[index, h, pl.ds(row, 16), :] = bottom

    def joined(read):
        return jnp.concatenate([read(k, h) for k in range(KPART) for h in range(halves)], axis=1)

    def apply(slot, j, region, high, low, part):
        first = part * KPART
        group = first // 4
        left = joined(lambda k, h: lhs[slot, first + k, j * halves + h])
        at = pl.ds(pl.multiple_of(region * TILE_I, TILE_I), TILE_I)
        acc[group, :, at] += dot_nt(left, joined(lambda k, h: high[first + k, h]))
        acc[group, 0:SPAN, at] += dot_nt(left[0:SPAN], joined(lambda k, h: low[first + k, h]))

    def step(index, carry):
        slot, region = items[0, index], items[1, index]
        before = jnp.maximum(index - 1, 0)
        slot_before, region_before = items[0, before], items[1, before]

        def first(part, c):
            evaluate(slot, 0, region, high0, low0, part)
            apply(slot_before, 1, region_before, high1, low1, part)
            return c

        def second(part, c):
            evaluate(slot, 1, region, high1, low1, part)
            apply(slot, 0, region, high0, low0, part)
            return c

        lax.fori_loop(0, 16 // KPART, first, 0)
        lax.fori_loop(0, 16 // KPART, second, 0)
        return carry

    lax.fori_loop(0, total, step, 0)

    @pl.when(total > 0)
    def _():
        slot, region = items[0, total - 1], items[1, total - 1]

        def rest(part, c):
            apply(slot, 1, region, high1, low1, part)
            return c

        lax.fori_loop(0, 16 // KPART, rest, 0)


def near_call(metas, sources, payloads, acc, last=False):
    count = len(payloads)
    panels = payloads[0].shape[1]
    tiles = panels // LANES
    regions = 3 if last else 2
    shape = jax.ShapeDtypeStruct((4, SPAN, 2 * TILE_I), F32)
    anywhere = pl.BlockSpec(memory_space=pl.ANY)
    arguments = [*metas, *payloads] + ([] if acc is None else [acc])
    return pl.pallas_call(
        lambda *refs: near_kernel(sources, acc is not None, last, *refs),
        out_shape=(shape, jax.ShapeDtypeStruct((4, SPAN, TILE_I), F32)) if last else shape,
        in_specs=[anywhere] * len(arguments),
        out_specs=(anywhere, anywhere) if last else anywhere,
        input_output_aliases={} if acc is None or last else {len(arguments) - 1: 0},
        scratch_shapes=[
            pltpu.VMEM((count,) + payloads[0].shape, F32),
            pltpu.VMEM((2, META, panels), F32),
            pltpu.VMEM((3, regions * TILE_I, LANES), F32),
            pltpu.VMEM((4, 2 * SPAN, regions * TILE_I), F32),
            pltpu.VMEM((count, 16, tiles, 2 * SPAN, LANES), BF16),
            pltpu.VMEM((count, tiles, META, LANES), F32),
        ]
        + [pltpu.VMEM((16, TILE_J // LANES, TILE_I, LANES), BF16)] * 4
        + [pltpu.SMEM((2, 16), jnp.int32), pltpu.SemaphoreType.DMA((4 + count,))],
        compiler_params=pltpu.CompilerParams(vmem_limit_bytes=NEAR_LIMIT),
        cost_estimate=pl.CostEstimate(
            flops=count * 2 * 32768 * 256 * 256, bytes_accessed=4 << 20, transcendentals=0
        ),
        name="near",
    )(*arguments)


def final_kernel(keep, received, incident, out):
    core = lax.rem(lax.axis_index("clus"), 2)
    half = math.sqrt(0.5)
    for local in range(0, 2 * TILE_I, LANES):
        near_half = local < TILE_I
        side = core if near_half else 1 - core
        row = pl.multiple_of(side * TILE_I + local % TILE_I, LANES)
        at = pl.ds(row, LANES)
        parts = []
        for group in range(4):
            whole = keep[group, :, local : local + LANES]
            if not near_half:
                whole = whole + received[group, :, local - TILE_I : local - TILE_I + LANES]
            parts.append([whole[n * COLS : (n + 1) * COLS] for n in range(4)])
        first, second, third, fourth = parts
        plus = [first[n] + second[n] for n in range(4)] + [first[n] - second[n] for n in range(4)]
        minus = [None] * 8
        for m in range(2):
            sum_r, sum_i = third[m] + fourth[m], third[m + 2] + fourth[m + 2]
            gap_r, gap_i = third[m] - fourth[m], third[m + 2] - fourth[m + 2]
            minus[m], minus[m + 4] = sum_r, sum_i
            minus[m + 2] = half * (gap_r + gap_i)
            minus[m + 6] = half * (gap_i - gap_r)
        steps = [None] * 16
        for m in range(8):
            low = plus[m] + minus[m]
            high = plus[m] - minus[m]
            for n, value in ((-m % 16, low), ((-m - 8) % 16, high)):
                steps[n] = value * (0.25 * RADIUS ** (-n))
        potential = jnp.concatenate(steps, axis=0).T
        out[0, at, :] = incident[0, at, :] - potential


def residual(density, positions, area, incident, pair_list, pair_count):
    devices = lax.axis_size("clus")
    panels = positions.shape[2]
    pairs = (pair_list, pair_count)
    vmem = pl.BlockSpec(memory_space=pltpu.VMEM)
    smem = pl.BlockSpec(memory_space=pltpu.SMEM)
    payload = pl.pallas_call(
        fold_kernel,
        out_shape=jax.ShapeDtypeStruct((16 * COLS + META, panels), F32),
        grid=(panels // FOLD,),
        in_specs=[
            pl.BlockSpec((1, FOLD, density.shape[2]), lambda p: (0, p, 0)),
            pl.BlockSpec((1, FOLD), lambda p: (0, p)),
            pl.BlockSpec((3, 1, FOLD), lambda p: (0, 0, p)),
            smem,
            smem,
        ],
        out_specs=pl.BlockSpec((16 * COLS + META, FOLD), lambda p: (0, p)),
        scratch_shapes=[pltpu.VMEM((density.shape[2], FOLD), F32)],
        compiler_params=pltpu.CompilerParams(vmem_limit_bytes=VMEM_LIMIT),
        name="fold",
    )(density, area, positions.transpose(1, 0, 2), *pairs)

    def route(value, move, members=lambda k: True):
        pairs_of = [(k, move(k) % devices) for k in range(devices) if members(k)]
        return lax.ppermute(value, "clus", pairs_of)

    def swap(value):
        return route(value, lambda k: k ^ 1)

    partner = swap(payload)
    ahead = route(payload, lambda k: k - 2)
    far = route(payload, lambda k: k - 3 if k % 2 == 0 else k + 3)
    behind = route(payload, lambda k: k + 2)
    metas = (payload, partner)
    acc = near_call(metas, ((0, 1), (1, -1)), (payload, partner), None)
    ahead_other = swap(ahead)
    acc = near_call(metas, ((2, 1), (3, -1)), (ahead, ahead_other), acc)
    behind_other = swap(behind)
    keep, send = near_call(
        metas, ((-2, 1), (-1, -1), (-3, FAR)), (behind, behind_other, far), acc, True
    )
    received = swap(send)
    return pl.pallas_call(
        final_kernel,
        out_shape=jax.ShapeDtypeStruct(incident.shape, F32),
        in_specs=[vmem] * 3,
        out_specs=vmem,
        compiler_params=pltpu.CompilerParams(vmem_limit_bytes=VMEM_LIMIT),
        name="final",
    )(keep, received, incident)


def solution(mesh):
    spec3 = P(("parts", "clus"), None, None)
    in_specs = (spec3, spec3, P(("parts", "clus"), None), spec3, P(("parts", "clus")), P(("parts", "clus")))
    return jax.shard_map(residual, mesh=mesh, in_specs=in_specs, out_specs=spec3, check_vma=False)
```
